32 devices in a mesh: group: 2 (over x), tm: 16 (over z, y, core).
Axes of the slice: x: 2, y: 2, z: 4, core: 2. Of those that a mesh axis runs over, the one named last changes fastest.
Arguments:
- state: bfloat16 [32, 512, 512], P(('group', 'tm')), parts along dimension 0, may hold values from -6 to 6
- noise: bfloat16 [32, 512, 512], P(('group', 'tm')), parts along dimension 0, may hold values from -6 to 6
- gain_first: float32 [512], replicated, may hold values from 0.1 to 1.9
- gain_second: float32 [512], replicated, may hold values from 0.1 to 1.9
- self_query: bfloat16 [512, 512], replicated, may hold values from -16 to 16, as said below
- self_key: bfloat16 [512, 512], replicated, may hold values from -8 to 8, as said below
- self_value: bfloat16 [512, 512], replicated, may hold values from -0.25 to 0.25
- self_out: bfloat16 [512, 512], replicated, may hold values from -0.25 to 0.25
- cross_query: bfloat16 [512, 512], replicated, may hold values from -16 to 16, as said below
- cross_key: bfloat16 [512, 512], replicated, may hold values from -8 to 8, as said below
- cross_value: bfloat16 [512, 512], replicated, may hold values from -0.25 to 0.25
- cross_out: bfloat16 [512, 512], replicated, may hold values from -0.25 to 0.25
- obs_operator: bfloat16 [512, 128], replicated, may hold values from -0.25 to 0.25
- obs_owner: int32 [8192, 1], P(('group', 'tm')), parts along dimension 0, may hold values from 0 to 15; in each aligned block of 256 rows (0 to 255, 256 to 511, ...) at most 16 rows name the same one
- obs_row: int32 [8192], P(('group', 'tm')), parts along dimension 0, may hold values from 0 to 511
- obs_value: bfloat16 [8192, 128], P(('group', 'tm')), parts along dimension 0, may hold values from -6 to 6
Outputs:
- drift: bfloat16 [32, 512, 512], P(('group', 'tm')), parts along dimension 0
- updated: bfloat16 [32, 512, 512], P(('group', 'tm')), parts along dimension 0
The draws below stay inside these ranges and needn't reach their ends.
There are 2 independent parts, one for each index of `group`. The reference program is written for one: setup_inputs(seed, part) draws one part's arguments, and reference() takes and returns one part's arrays. A program takes and returns all parts, laid end to end along the dimension named above; an argument that names none is the same for every part. Nothing has to cross between parts.
Inputs may be any that keep to these rules, and one draw needn't show every extreme that they name: `obs_owner`: among the 256 observations held by one index of tm, at most 16 refer to any one state, and some state receives exactly 16 of them. `self_query`: a query projection. `self_key`: a key projection. `cross_query`: a query projection. `cross_key`: a key projection.
All inputs are finite; a program needn't handle non-finite values.
Results may differ from the reference program's by a relative error of at most 0.014.
The reference program's roundings to bfloat16 on the way count: a program that leaves them out, or rounds other values in their place, can miss the bound.
Values may be sent and summed in bfloat16 or wider, within the bound.
A program may use at most 128 MiB of HBM per device.

```python
import math
import jax
import jax.numpy as jnp
import numpy as np
from jax import lax

D = 512
HEADS = 16
OW = 128
TOK_DEV = 512
OBS_DEV = 256
CAP = 16
STATES = 16
OBS = 4096


def shared_matrix(key, which):
    return jax.random.normal(jax.random.fold_in(key, which), (D, D), jnp.float32) * D ** (-0.5)


def tied_query(key, own):
    base = shared_matrix(key, own)
    return base


def draw_self_key(key, part):
    return shared_matrix(key, 11).astype(jnp.bfloat16)


def draw_self_query(key, part):
    return tied_query(key, 12).astype(jnp.bfloat16)


def draw_cross_key(key, part):
    return shared_matrix(key, 21).astype(jnp.bfloat16)


def draw_cross_query(key, part):
    return tied_query(key, 22).astype(jnp.bfloat16)


def plant(values, own_key, smallest, high):
    place = [jax.random.randint(jax.random.fold_in(own_key, axis), (), 0, length) for axis, length in enumerate(values.shape)]
    widest = values.shape.index(max(values.shape))
    beside = place[:widest] + [(place[widest] + 1) % values.shape[widest]] + place[widest + 1:]
    return values.at[tuple(place)].set(smallest).at[tuple(beside)].set(high)


def block_scale(own_key, extent, split, least, high):
    loudness, own = 1.0, jax.random.fold_in(own_key, 6)
    for dim, blocks in split:
        draws = jnp.exp(jax.random.uniform(jax.random.fold_in(own, dim), (blocks,), jnp.float32, least / len(split), high / len(split)))
        loudness = loudness * jnp.repeat(draws, extent[dim] // blocks).reshape([-1 if axis == dim else 1 for axis in range(len(extent))])
    return loudness


def assign_block(key, own, number, rows, count, top, most, slope):
    sequence = jax.random.permutation(key, count)
    packed, usual = load_shares(count, rows * top, most, slope, True), load_shares(count, rows * top, most, slope, False)
    places = jnp.arange(count)

    def named(lengths, turn):
        used = int((lengths > 0).sum())
        fixed = max(1, used // 4)
        moved = fixed + (places - fixed + turn * (used - fixed)) % max(1, count - fixed)
        return jnp.zeros((count,), jnp.int32).at[sequence[jnp.where(places < fixed, places, moved)]].set(jnp.asarray(lengths, jnp.int32))

    lengths = jnp.where(number % 4 == 0, named(packed, number // 4), named(usual, number - number // 4 - 1))
    mixed = jax.random.permutation(jax.random.fold_in(own, 3), count)
    giver, sink = mixed[0:count // 2 * 2:2], mixed[1:count // 2 * 2:2]
    room = jnp.minimum(lengths[giver] - 1, most - lengths[sink]) // 2
    room = jnp.where((giver == sequence[0]) | (sink == sequence[0]) | (lengths[sink] == 0), 0, jnp.maximum(room, 0))
    moved = jax.random.randint(jax.random.fold_in(own, 4), (count // 2,), 0, 1 << 20) % (room + 1)
    lengths = lengths.at[giver].add(-moved).at[sink].add(moved)
    items = jnp.searchsorted(jnp.cumsum(lengths), jnp.arange(rows * top), side="right").astype(jnp.int32)
    listing = items.reshape(top, rows).T
    listing = listing[jax.random.permutation(jax.random.fold_in(own, 1), rows)]
    turn = jax.random.randint(jax.random.fold_in(own, 2), (rows, 1), 0, top)
    return jnp.take_along_axis(listing, (jnp.arange(top)[None, :] + turn) % top, axis=1)


def load_shares(amount, total, reach, lean, full):
    weights = [(1 << 20) // math.isqrt(rank ** lean) + 1 for rank in range(1, amount + 1)]
    largest = reach if full else min(reach, max(-(-total // amount), total * weights[0] // sum(weights)))
    least = 1 if total - largest >= amount - 1 else 0
    holding, rest = [largest] + [least] * (amount - 1), total - largest - least * (amount - 1)
    while rest > 0:
        free = [i for i in range(1, amount) if holding[i] < largest] or [i for i in range(1, amount) if holding[i] < reach]
        mass, budget = sum([weights[i] for i in free]), rest
        for i in free:
            extra = min(reach - holding[i], max(1, budget * weights[i] // mass), rest)
            holding[i] = holding[i] + extra
            rest = rest - extra
    return np.array(holding)


def gaussian(own_key, shape, spread, reach, shards=(), held_as=jnp.bfloat16):
    values = jax.random.normal(own_key, shape, jnp.float32) * spread
    if len(shards) > 0:
        values = block_scale(own_key, shape, shards, -0.22, 0.18) * values
    return jnp.clip(values, min=-reach, max=reach).astype(held_as)


def setup_inputs(seed: int = 0, part: int = 0) -> dict:
    seeds = jax.random.split(jax.random.key(seed), 17)
    part_splits = jax.random.split(jax.random.fold_in(seeds[16], part), 17)
    state = gaussian(part_splits[0], (STATES, TOK_DEV, D), 1.0, 6.0, ((0, 16),))
    noise = gaussian(part_splits[1], (STATES, TOK_DEV, D), 1.0, 6.0, ((0, 16),))
    gain_first = jnp.clip(1.0 + 0.18 * jax.random.normal(seeds[2], (D,), jnp.float32), 0.1, 1.9)
    gain_second = jnp.clip(1.0 + 0.18 * jax.random.normal(seeds[3], (D,), jnp.float32), 0.1, 1.9)
    self_query = draw_self_query(jax.random.fold_in(seeds[16], 71), part)
    self_key = draw_self_key(jax.random.fold_in(seeds[16], 71), part)
    self_value = gaussian(seeds[6], (D, D), D ** -0.5, 0.25)
    self_out = gaussian(seeds[7], (D, D), D ** -0.5, 0.25)
    cross_query = draw_cross_query(jax.random.fold_in(seeds[16], 71), part)
    cross_key = draw_cross_key(jax.random.fold_in(seeds[16], 71), part)
    cross_value = gaussian(seeds[10], (D, D), D ** -0.5, 0.25)
    cross_out = gaussian(seeds[11], (D, D), D ** -0.5, 0.25)
    obs_operator = gaussian(seeds[12], (D, OW), D ** -0.5, 0.25)
    obs_owner_keys = jax.random.split(jax.random.fold_in(part_splits[13], 1), OBS // OBS_DEV)
    obs_owner_turns = jax.random.permutation(jax.random.fold_in(part_splits[13], 3), OBS // OBS_DEV)
    obs_owner = jax.vmap(lambda own, number: assign_block(jax.random.fold_in(part_splits[13], 2), own, number, OBS_DEV, STATES, 1, CAP, 2))(obs_owner_keys, obs_owner_turns).reshape((OBS, 1))
    obs_row = plant(jax.random.randint(part_splits[14], (OBS,), 0, TOK_DEV), jax.random.fold_in(part_splits[14], 1), 0, TOK_DEV - 1).astype(jnp.int32)
    obs_value = gaussian(part_splits[15], (OBS, OW), 1.0, 6.0, ((0, 16),))
    return {"state": state, "noise": noise, "gain_first": gain_first, "gain_second": gain_second, "self_query": self_query, "self_key": self_key, "self_value": self_value, "self_out": self_out, "cross_query": cross_query, "cross_key": cross_key, "cross_value": cross_value, "cross_out": cross_out, "obs_operator": obs_operator, "obs_owner": obs_owner, "obs_row": obs_row, "obs_value": obs_value}


step_size = 0.1
inv_var = 2.0

def rms_norm(vector, gain_vector):
    vector = vector.astype(jnp.float32)
    return vector * lax.rsqrt(lax.optimization_barrier(jnp.mean(vector * vector, axis=-1, keepdims=True)) + 1e-05) * gain_vector.astype(jnp.float32)

def attend(query, key_rows, value_rows, allowed):
    head_size = D // HEADS
    qf = query.astype(jnp.float32).reshape(query.shape[0], HEADS, head_size)
    kf = key_rows.astype(jnp.float32).reshape(key_rows.shape[0], HEADS, head_size)
    vf = value_rows.astype(jnp.float32).reshape(value_rows.shape[0], HEADS, head_size)
    scores = jnp.einsum('qhd,khd->hqk', qf, kf) * head_size ** (-0.5)
    scores = jnp.where(allowed[None, None, :], scores, jnp.float32(-1e+30))
    largest = lax.optimization_barrier(jnp.max(scores, axis=-1, keepdims=True))
    exponent = jnp.exp(scores - largest)
    weights = (exponent / lax.optimization_barrier(jnp.sum(exponent, axis=-1, keepdims=True))).astype(jnp.bfloat16)
    result = jnp.einsum('hqk,khd->qhd', weights.astype(jnp.float32), vf)
    return result.reshape(query.shape[0], D).astype(jnp.bfloat16)

def project(array, matrix):
    return jnp.einsum('std,de->ste', array.astype(jnp.float32), matrix.astype(jnp.float32))

def reference(state, noise, gain_first, gain_second, self_query, self_key, self_value, self_out, cross_query, cross_key, cross_value, cross_out, obs_operator, obs_owner, obs_row, obs_value):
    normed = rms_norm(state, gain_first).astype(jnp.bfloat16)
    queries = project(normed, self_query).astype(jnp.bfloat16)
    keys_self = project(normed, self_key).astype(jnp.bfloat16)
    values_self = project(normed, self_value).astype(jnp.bfloat16)
    every = jnp.ones((TOK_DEV,), bool)
    attended = lax.map(lambda trio: attend(trio[0], trio[1], trio[2], every), (queries, keys_self, values_self))
    middle = (state.astype(jnp.float32) + project(attended, self_out)).astype(jnp.bfloat16)
    lifted = rms_norm(middle, gain_second).astype(jnp.bfloat16)
    cross_q = project(lifted, cross_query).astype(jnp.bfloat16)
    cross_k = project(normed, cross_key).astype(jnp.bfloat16)
    cross_v = project(normed, cross_value).astype(jnp.bfloat16)
    blank = jnp.zeros((1, TOK_DEV, D), jnp.bfloat16)
    padded_k = jnp.concatenate([blank, cross_k, blank], axis=0)
    padded_v = jnp.concatenate([blank, cross_v, blank], axis=0)

    def cross_one(position):
        before_k = lax.dynamic_index_in_dim(padded_k, position, 0, keepdims=False)
        after_k = lax.dynamic_index_in_dim(padded_k, position + 2, 0, keepdims=False)
        before_v = lax.dynamic_index_in_dim(padded_v, position, 0, keepdims=False)
        after_v = lax.dynamic_index_in_dim(padded_v, position + 2, 0, keepdims=False)
        allowed = jnp.concatenate([jnp.full((TOK_DEV,), position > 0), jnp.full((TOK_DEV,), position < STATES - 1)])
        query = lax.dynamic_index_in_dim(cross_q, position, 0, keepdims=False)
        return attend(query, jnp.concatenate([before_k, after_k]), jnp.concatenate([before_v, after_v]), allowed)
    crossed = lax.map(cross_one, jnp.arange(STATES, dtype=jnp.int32))
    score = middle.astype(jnp.float32) + project(crossed, cross_out)
    owners = obs_owner[:, 0]
    picked = state[owners, obs_row]
    predicted = jnp.dot(picked, obs_operator, preferred_element_type=jnp.float32)
    misfit = inv_var * (obs_value.astype(jnp.float32) - predicted)
    token_misfit = jnp.zeros((STATES, TOK_DEV, OW), jnp.float32).at[owners, obs_row].add(misfit).astype(jnp.bfloat16)
    gradient = jnp.einsum('sto,do->std', token_misfit.astype(jnp.float32), obs_operator.astype(jnp.float32))
    combined = score + gradient
    drift = combined.astype(jnp.bfloat16)
    updated = (state.astype(jnp.float32) + step_size * combined + math.sqrt(2.0 * step_size) * noise.astype(jnp.float32)).astype(jnp.bfloat16)
    return (drift, updated)
```

```python
import functools
import math

import jax
import jax.numpy as jnp
from jax import lax
from jax.experimental import pallas as pl
from jax.experimental.pallas import tpu as pltpu
from jax.sharding import PartitionSpec as P

HEADS = 16
CAP = 16
LANES = 128

step_size = 0.1
inv_var = 2.0
MESH = pl.DeviceIdType.MESH
NT = (((1,), (1,)), ((), ()))
TN = (((0,), (0,)), ((), ()))


def matmul(a, b):
    return jnp.dot(a, b, preferred_element_type=jnp.float32)


def rms_norm(rows, gain):
    rows = rows.astype(jnp.float32)
    scale = lax.rsqrt(jnp.mean(rows * rows, axis=-1, keepdims=True) + 1e-05)
    return (rows * scale * gain).astype(jnp.bfloat16)


def attend_block(q_ref, kv_refs, out_ref, lanes, head_size):
    q_block = q_ref[:, lanes]
    lane = lax.broadcasted_iota(jnp.int32, (1, LANES), 1) // head_size
    factor = head_size ** (-0.5) * math.log2(math.e)
    total = None
    for h in range(LANES // head_size):
        own = lane == h
        q_head = jnp.where(own, q_block, jnp.zeros_like(q_block))
        scores = [
            lax.dot_general(q_head, k[:, lanes], NT, preferred_element_type=jnp.float32)
            for k, _ in kv_refs
        ]
        largest = functools.reduce(
            jnp.maximum, [jnp.max(s, axis=-1, keepdims=True) for s in scores]
        )
        for s, (_, v) in zip(scores, kv_refs):
            weights = jnp.exp2(((s - largest) * factor).astype(jnp.bfloat16))
            v_block = v[:, lanes]
            v_head = jnp.where(own, v_block, jnp.zeros_like(v_block))
            ones = jnp.broadcast_to(own, v_block.shape).astype(jnp.bfloat16)
            part = matmul(weights, jnp.concatenate([v_head, ones], axis=1))
            total = part if total is None else total + part
    out_ref[:, lanes] = (total[:, :LANES] / total[:, LANES:]).astype(jnp.bfloat16)


def attend(q_ref, kv_refs, out_ref):
    width = q_ref.shape[1]
    head_size = width // HEADS

    @pl.loop(0, width // LANES)
    def _(block):
        lanes = pl.ds(pl.multiple_of(block * LANES, LANES), LANES)
        attend_block(q_ref, kv_refs, out_ref, lanes, head_size)


def kernel(
    n,
    state_hbm, noise_hbm, gain_first, gain_second,
    wq_hbm, wk_hbm, wv_hbm, wo_hbm, cq_hbm, ck_hbm, cv_hbm, co_hbm,
    operator, owner_ref, row_ref, value_ref,
    drift_ref, updated_ref,
    x, noise, wq, wk, wv, wo, cq, ck, cv, co,
    before, after, normed, q, k, v, att, mid, kb, vb, ka, va, message, inbox,
    load_sem, near_send, near_recv, obs_send, obs_recv,
):
    me = lax.axis_index("tm")
    token_count = x.shape[0]
    obs_count = value_ref.shape[0]

    sources = [state_hbm, wq_hbm, wk_hbm, wv_hbm, wo_hbm, cq_hbm, ck_hbm, cv_hbm, co_hbm, noise_hbm]
    targets = [x, wq, wk, wv, wo, cq, ck, cv, co, noise]
    loads = [pltpu.make_async_copy(s, t, load_sem.at[i]) for i, (s, t) in enumerate(zip(sources, targets))]
    for load in loads:
        load.start()
    load_x, load_wq, load_wk, load_wv, load_wo, load_cq, load_ck, load_cv, load_co, load_noise = loads

    barrier = pltpu.get_barrier_semaphore()

    @pl.loop(1, n)
    def _(offset):
        peer = lax.rem(me + offset, n)
        pl.semaphore_signal(barrier, inc=1, device_id={"tm": peer}, device_id_type=MESH)

    owner = owner_ref[...]
    onehot = lax.broadcasted_iota(jnp.int32, (n, obs_count), 0) == owner
    earlier = lax.broadcasted_iota(jnp.int32, (obs_count, obs_count), 0) <= lax.broadcasted_iota(
        jnp.int32, (obs_count, obs_count), 1
    )
    running = matmul(onehot.astype(jnp.bfloat16), earlier.astype(jnp.bfloat16))
    place = jnp.sum(jnp.where(onehot, running, 0.0), axis=0, keepdims=True) - 1.0
    destination = owner * CAP + place.astype(jnp.int32)
    routed = lax.broadcasted_iota(jnp.int32, (n * CAP, obs_count), 0) == destination
    values = matmul(routed.astype(jnp.bfloat16), value_ref[...])
    row = row_ref[...]
    high = jnp.sum(jnp.where(routed, ((row >> 8) + 1).astype(jnp.float32), 0.0), axis=1, keepdims=True) - 1.0
    low = jnp.sum(jnp.where(routed, (row & 255).astype(jnp.float32), 0.0), axis=1, keepdims=True)
    side = lax.broadcasted_iota(jnp.int32, (n * CAP, LANES), 1)
    codes = jnp.where(side == 0, high, low)
    message[...] = (
        jnp.concatenate([values, codes], axis=1).astype(jnp.bfloat16).reshape(message.shape)
    )

    load_x.wait()
    normed[...] = rms_norm(x[...], gain_first[...])

    pl.semaphore_wait(barrier, n - 1)
    to_next = pltpu.make_async_remote_copy(
        src_ref=state_hbm, dst_ref=before, send_sem=near_send.at[0], recv_sem=near_recv.at[0],
        device_id={"tm": lax.rem(me + 1, n)}, device_id_type=MESH,
    )
    to_last = pltpu.make_async_remote_copy(
        src_ref=state_hbm, dst_ref=after, send_sem=near_send.at[1], recv_sem=near_recv.at[1],
        device_id={"tm": lax.rem(me + n - 1, n)}, device_id_type=MESH,
    )

    @pl.when(me < n - 1)
    def _():
        to_next.start()

    @pl.when(me > 0)
    def _():
        to_last.start()

    load_wq.wait()
    q[...] = matmul(normed[...], wq[...]).astype(jnp.bfloat16)
    load_wk.wait()
    k[...] = matmul(normed[...], wk[...]).astype(jnp.bfloat16)
    load_wv.wait()
    v[...] = matmul(normed[...], wv[...]).astype(jnp.bfloat16)

    def observation_copy(offset):
        peer = lax.rem(me + offset, n)
        return pltpu.make_async_remote_copy(
            src_ref=message.at[peer], dst_ref=inbox.at[me],
            send_sem=obs_send.at[offset], recv_sem=obs_recv.at[offset],
            device_id={"tm": peer}, device_id_type=MESH,
        )

    @pl.loop(1, n)
    def _(offset):
        observation_copy(offset).start()

    attend(q, [(k, v)], att)
    load_wo.wait()
    middle = (x[...].astype(jnp.float32) + matmul(att[...], wo[...])).astype(jnp.bfloat16)
    mid[...] = middle
    lifted = rms_norm(middle, gain_second[...])
    load_cq.wait()
    q[...] = matmul(lifted, cq[...]).astype(jnp.bfloat16)

    @pl.when(me > 0)
    def _():
        to_next.wait_recv()

    @pl.when(me < n - 1)
    def _():
        to_last.wait_recv()

    @pl.when(me == 0)
    def _():
        before[...] = after[...]

    @pl.when(me == n - 1)
    def _():
        after[...] = before[...]

    load_ck.wait()
    load_cv.wait()
    for rows, keys, vals in ((before, kb, vb), (after, ka, va)):
        near = rms_norm(rows[...], gain_first[...])
        keys[...] = matmul(near, ck[...]).astype(jnp.bfloat16)
        vals[...] = matmul(near, cv[...]).astype(jnp.bfloat16)
    attend(q, [(kb, vb), (ka, va)], att)

    @pl.when(me < n - 1)
    def _():
        to_next.wait_send()

    @pl.when(me > 0)
    def _():
        to_last.wait_send()

    @pl.loop(1, n)
    def _(offset):
        observation_copy(offset).wait()

    inbox[me] = message[me]

    arrived = inbox[...].reshape(n * CAP, 2 * LANES)
    codes_in = arrived[:, LANES:].astype(jnp.float32)
    rows_in = (codes_in[:, 0:1] * 256.0 + codes_in[:, 1:2]).astype(jnp.int32)
    hit = (rows_in == lax.broadcasted_iota(jnp.int32, (n * CAP, token_count), 1)).astype(jnp.bfloat16)
    gathered = lax.dot_general(
        hit,
        jnp.concatenate([arrived[:, :LANES], jnp.ones((n * CAP, LANES), jnp.bfloat16)], axis=1),
        TN, preferred_element_type=jnp.float32,
    )
    predicted = matmul(x[...], operator[...])
    token_misfit = (
        inv_var * (gathered[:, :LANES] - gathered[:, LANES:] * predicted)
    ).astype(jnp.bfloat16)
    gradient = lax.dot_general(token_misfit, operator[...], NT, preferred_element_type=jnp.float32)
    load_co.wait()
    combined = mid[...].astype(jnp.float32) + matmul(att[...], co[...]) + gradient
    drift_ref[...] = combined.astype(jnp.bfloat16)
    load_noise.wait()
    updated_ref[...] = (
        x[...].astype(jnp.float32)
        + step_size * combined
        + math.sqrt(2.0 * step_size) * noise[...].astype(jnp.float32)
    ).astype(jnp.bfloat16)


def per_device(
    state, noise, gain_first, gain_second,
    self_query, self_key, self_value, self_out,
    cross_query, cross_key, cross_value, cross_out,
    obs_operator, obs_owner, obs_row, obs_value,
):
    n = lax.axis_size("tm")
    tokens = state[0]
    token_count, width = tokens.shape
    obs_count, channels = obs_value.shape
    hbm = pl.BlockSpec(memory_space=pl.ANY)
    vmem = pl.BlockSpec(memory_space=pltpu.VMEM)
    rows = pltpu.VMEM((token_count, width), jnp.bfloat16)
    square = pltpu.VMEM((width, width), jnp.bfloat16)
    box = pltpu.VMEM((n, CAP, channels + LANES), jnp.bfloat16)
    out = jax.ShapeDtypeStruct((token_count, width), jnp.bfloat16)
    drift, updated = pl.pallas_call(
        functools.partial(kernel, n),
        name="langevin",
        out_shape=(out, out),
        in_specs=[hbm, hbm, vmem, vmem] + [hbm] * 8 + [vmem] * 4,
        out_specs=(vmem, vmem),
        scratch_shapes=[rows, rows] + [square] * 8 + [rows] * 12 + [
            box, box,
            pltpu.SemaphoreType.DMA((10,)),
            pltpu.SemaphoreType.DMA((2,)),
            pltpu.SemaphoreType.DMA((2,)),
            pltpu.SemaphoreType.DMA((n,)),
            pltpu.SemaphoreType.DMA((n,)),
        ],
        compiler_params=pltpu.CompilerParams(
            collective_id=0, has_side_effects=True, vmem_limit_bytes=56 * 1024 * 1024
        ),
    )(
        tokens, noise[0], gain_first[None, :], gain_second[None, :],
        self_query, self_key, self_value, self_out,
        cross_query, cross_key, cross_value, cross_out,
        obs_operator, obs_owner.reshape(1, obs_count), obs_row.reshape(1, obs_count), obs_value,
    )
    return (drift[None], updated[None])


def solution(mesh):
    split = P(("group", "tm"), None, None)
    return jax.shard_map(
        per_device,
        mesh=mesh,
        in_specs=(split, split) + (P(),) * 11 + (
            P(("group", "tm"), None),
            P(("group", "tm")),
            P(("group", "tm"), None),
        ),
        out_specs=(split, split),
        check_vma=False,
    )
```

```python
import functools
import math

import jax
import jax.numpy as jnp
from jax import lax
from jax.experimental import pallas as pl
from jax.experimental.pallas import tpu as pltpu
from jax.sharding import PartitionSpec as P

HEADS = 16
CAP = 16
CHUNK = 256
LANES = 128

step_size = 0.1
inv_var = 2.0
MESH = pl.DeviceIdType.MESH
NT = (((1,), (1,)), ((), ()))
TN = (((0,), (0,)), ((), ()))


def matmul(a, b):
    return jnp.dot(a, b, preferred_element_type=jnp.float32)


def rms_norm(rows, gain):
    rows = rows.astype(jnp.float32)
    scale = lax.rsqrt(jnp.mean(rows * rows, axis=-1, keepdims=True) + 1e-05)
    return (rows * scale * gain).astype(jnp.bfloat16)


def attend(q_ref, kv_refs, out_ref, score_refs, peak_refs):
    token_count, width = q_ref.shape
    head_size = width // HEADS
    per_block = LANES // head_size
    blocks = width // LANES
    factor = head_size ** (-0.5) * math.log2(math.e)
    lane = lax.broadcasted_iota(jnp.int32, (1, LANES), 1) // head_size
    ones = jnp.ones((16, CHUNK), jnp.bfloat16)
    chunks = [(k, v, c * CHUNK) for k, v in kv_refs for c in range(token_count // CHUNK)]

    def head_queries(block, h):
        lanes = pl.ds(pl.multiple_of(block * LANES, LANES), LANES)
        q_block = q_ref[:, lanes]
        return jnp.where(lane == h, q_block, jnp.zeros_like(q_block)), lanes

    def score(index, q_head, lanes, slot, peak):
        k, _, start = chunks[index]
        part = lax.dot_general(
            k[start : start + CHUNK, lanes], q_head, NT, preferred_element_type=jnp.float32
        )
        score_refs[slot][index * CHUNK : (index + 1) * CHUNK, :] = part
        top = jnp.max(part.reshape(CHUNK // 8, 8, token_count), axis=0)
        return top if peak is None else jnp.maximum(peak, top)

    def stage(block, h, next_block, next_h):
        slot, next_slot = h % 2, next_h % 2
        q_head, lanes = head_queries(next_block, next_h)
        largest = jnp.max(peak_refs[slot][...], axis=0, keepdims=True)
        features = pl.ds(pl.multiple_of(block * LANES + h * head_size, head_size), head_size)
        total, peak = None, None
        for index, (_, v, start) in enumerate(chunks):
            peak = score(index, q_head, lanes, next_slot, peak)
            part = score_refs[slot][index * CHUNK : (index + 1) * CHUNK, :]
            weights = jnp.exp2(((part - largest) * factor).astype(jnp.bfloat16))
            rows = jnp.concatenate([v[features, start : start + CHUNK], ones], axis=0)
            part = matmul(rows, weights)
            total = part if total is None else total + part
        peak_refs[next_slot][...] = peak
        out_ref[features, :] = (
            total[:head_size] / total[head_size : head_size + 1]
        ).astype(jnp.bfloat16)

    q_head, lanes = head_queries(0, 0)
    peak = None
    for index in range(len(chunks)):
        peak = score(index, q_head, lanes, 0, peak)
    peak_refs[0][...] = peak

    @pl.loop(0, blocks)
    def _(block):
        for h in range(per_block):
            if h < per_block - 1:
                stage(block, h, block, h + 1)
            else:
                stage(block, h, jnp.minimum(block + 1, blocks - 1), 0)


def kernel(
    n,
    state_hbm, noise_hbm, gain_first, gain_second,
    wq_hbm, wk_hbm, wv_hbm, wo_hbm, cq_hbm, ck_hbm, cv_hbm, co_hbm,
    operator, owner_ref, row_ref, value_ref,
    drift_ref, updated_ref,
    x, noise, wq, wk, wv, wo, cq, ck, cv, co,
    before, after, normed, q, k, v, att, mid, kb, vb, ka, va, message, inbox,
    scores_a, scores_b, peak_a, peak_b,
    load_sem, near_send, near_recv, obs_send, obs_recv,
):
    me = lax.axis_index("tm")
    token_count = x.shape[0]
    obs_count = value_ref.shape[0]

    sources = [state_hbm, wq_hbm, wk_hbm, wv_hbm, wo_hbm, cq_hbm, ck_hbm, cv_hbm, co_hbm, noise_hbm]
    targets = [x, wq, wk, wv, wo, cq, ck, cv, co, noise]
    loads = [pltpu.make_async_copy(s, t, load_sem.at[i]) for i, (s, t) in enumerate(zip(sources, targets))]
    for load in loads:
        load.start()
    load_x, load_wq, load_wk, load_wv, load_wo, load_cq, load_ck, load_cv, load_co, load_noise = loads

    barrier = pltpu.get_barrier_semaphore()

    @pl.loop(1, n)
    def _(offset):
        peer = lax.rem(me + offset, n)
        pl.semaphore_signal(barrier, inc=1, device_id={"tm": peer}, device_id_type=MESH)

    owner = owner_ref[...]
    onehot = lax.broadcasted_iota(jnp.int32, (n, obs_count), 0) == owner
    earlier = lax.broadcasted_iota(jnp.int32, (obs_count, obs_count), 0) <= lax.broadcasted_iota(
        jnp.int32, (obs_count, obs_count), 1
    )
    running = matmul(onehot.astype(jnp.bfloat16), earlier.astype(jnp.bfloat16))
    place = jnp.sum(jnp.where(onehot, running, 0.0), axis=0, keepdims=True) - 1.0
    destination = owner * CAP + place.astype(jnp.int32)
    routed = lax.broadcasted_iota(jnp.int32, (n * CAP, obs_count), 0) == destination
    values = matmul(routed.astype(jnp.bfloat16), value_ref[...])
    row = row_ref[...]
    high = jnp.sum(jnp.where(routed, ((row >> 8) + 1).astype(jnp.float32), 0.0), axis=1, keepdims=True) - 1.0
    low = jnp.sum(jnp.where(routed, (row & 255).astype(jnp.float32), 0.0), axis=1, keepdims=True)
    side = lax.broadcasted_iota(jnp.int32, (n * CAP, LANES), 1)
    codes = jnp.where(side == 0, high, low)
    message[...] = (
        jnp.concatenate([values, codes], axis=1).astype(jnp.bfloat16).reshape(message.shape)
    )

    load_x.wait()
    normed[...] = rms_norm(x[...], gain_first[...])

    pl.semaphore_wait(barrier, n - 1)
    to_next = pltpu.make_async_remote_copy(
        src_ref=state_hbm, dst_ref=before, send_sem=near_send.at[0], recv_sem=near_recv.at[0],
        device_id={"tm": lax.rem(me + 1, n)}, device_id_type=MESH,
    )
    to_last = pltpu.make_async_remote_copy(
        src_ref=state_hbm, dst_ref=after, send_sem=near_send.at[1], recv_sem=near_recv.at[1],
        device_id={"tm": lax.rem(me + n - 1, n)}, device_id_type=MESH,
    )

    @pl.when(me < n - 1)
    def _():
        to_next.start()

    @pl.when(me > 0)
    def _():
        to_last.start()

    load_wq.wait()
    q[...] = matmul(normed[...], wq[...]).astype(jnp.bfloat16)
    load_wk.wait()
    k[...] = matmul(normed[...], wk[...]).astype(jnp.bfloat16)
    load_wv.wait()
    v[...] = matmul(normed[...], wv[...]).astype(jnp.bfloat16).T

    def observation_copy(offset):
        peer = lax.rem(me + offset, n)
        return pltpu.make_async_remote_copy(
            src_ref=message.at[peer], dst_ref=inbox.at[me],
            send_sem=obs_send.at[offset], recv_sem=obs_recv.at[offset],
            device_id={"tm": peer}, device_id_type=MESH,
        )

    @pl.loop(1, n)
    def _(offset):
        observation_copy(offset).start()

    attend(q, [(k, v)], att, (scores_a, scores_b), (peak_a, peak_b))
    load_wo.wait()
    middle = (x[...].astype(jnp.float32) + lax.dot_general(att[...], wo[...], TN, preferred_element_type=jnp.float32)).astype(jnp.bfloat16)
    mid[...] = middle
    lifted = rms_norm(middle, gain_second[...])
    load_cq.wait()
    q[...] = matmul(lifted, cq[...]).astype(jnp.bfloat16)

    @pl.when(me > 0)
    def _():
        to_next.wait_recv()

    @pl.when(me < n - 1)
    def _():
        to_last.wait_recv()

    @pl.when(me == 0)
    def _():
        before[...] = after[...]

    @pl.when(me == n - 1)
    def _():
        after[...] = before[...]

    load_ck.wait()
    load_cv.wait()
    for rows, keys, vals in ((before, kb, vb), (after, ka, va)):
        near = rms_norm(rows[...], gain_first[...])
        keys[...] = matmul(near, ck[...]).astype(jnp.bfloat16)
        vals[...] = matmul(near, cv[...]).astype(jnp.bfloat16).T
    attend(q, [(kb, vb), (ka, va)], att, (scores_a, scores_b), (peak_a, peak_b))

    @pl.when(me < n - 1)
    def _():
        to_next.wait_send()

    @pl.when(me > 0)
    def _():
        to_last.wait_send()

    @pl.loop(1, n)
    def _(offset):
        observation_copy(offset).wait()

    inbox[me] = message[me]

    arrived = inbox[...].reshape(n * CAP, 2 * LANES)
    codes_in = arrived[:, LANES:].astype(jnp.float32)
    rows_in = (codes_in[:, 0:1] * 256.0 + codes_in[:, 1:2]).astype(jnp.int32)
    hit = (rows_in == lax.broadcasted_iota(jnp.int32, (n * CAP, token_count), 1)).astype(jnp.bfloat16)
    gathered = lax.dot_general(
        hit,
        jnp.concatenate([arrived[:, :LANES], jnp.ones((n * CAP, LANES), jnp.bfloat16)], axis=1),
        TN, preferred_element_type=jnp.float32,
    )
    predicted = matmul(x[...], operator[...])
    token_misfit = (
        inv_var * (gathered[:, :LANES] - gathered[:, LANES:] * predicted)
    ).astype(jnp.bfloat16)
    gradient = lax.dot_general(token_misfit, operator[...], NT, preferred_element_type=jnp.float32)
    load_co.wait()
    combined = mid[...].astype(jnp.float32) + lax.dot_general(att[...], co[...], TN, preferred_element_type=jnp.float32) + gradient
    drift_ref[...] = combined.astype(jnp.bfloat16)
    load_noise.wait()
    updated_ref[...] = (
        x[...].astype(jnp.float32)
        + step_size * combined
        + math.sqrt(2.0 * step_size) * noise[...].astype(jnp.float32)
    ).astype(jnp.bfloat16)


def per_device(
    state, noise, gain_first, gain_second,
    self_query, self_key, self_value, self_out,
    cross_query, cross_key, cross_value, cross_out,
    obs_operator, obs_owner, obs_row, obs_value,
):
    n = lax.axis_size("tm")
    tokens = state[0]
    token_count, width = tokens.shape
    obs_count, channels = obs_value.shape
    hbm = pl.BlockSpec(memory_space=pl.ANY)
    vmem = pl.BlockSpec(memory_space=pltpu.VMEM)
    rows = pltpu.VMEM((token_count, width), jnp.bfloat16)
    square = pltpu.VMEM((width, width), jnp.bfloat16)
    box = pltpu.VMEM((n, CAP, channels + LANES), jnp.bfloat16)
    scores = pltpu.VMEM((2 * token_count, token_count), jnp.float32)
    peak = pltpu.VMEM((8, token_count), jnp.float32)
    out = jax.ShapeDtypeStruct((token_count, width), jnp.bfloat16)
    drift, updated = pl.pallas_call(
        functools.partial(kernel, n),
        name="langevin",
        out_shape=(out, out),
        in_specs=[hbm, hbm, vmem, vmem] + [hbm] * 8 + [vmem] * 4,
        out_specs=(vmem, vmem),
        scratch_shapes=[rows, rows] + [square] * 8 + [rows] * 12 + [
            box, box,
            scores, scores, peak, peak,
            pltpu.SemaphoreType.DMA((10,)),
            pltpu.SemaphoreType.DMA((2,)),
            pltpu.SemaphoreType.DMA((2,)),
            pltpu.SemaphoreType.DMA((n,)),
            pltpu.SemaphoreType.DMA((n,)),
        ],
        compiler_params=pltpu.CompilerParams(
            collective_id=0, has_side_effects=True, vmem_limit_bytes=56 * 1024 * 1024
        ),
    )(
        tokens, noise[0], gain_first[None, :], gain_second[None, :],
        self_query, self_key, self_value, self_out,
        cross_query, cross_key, cross_value, cross_out,
        obs_operator, obs_owner.reshape(1, obs_count), obs_row.reshape(1, obs_count), obs_value,
    )
    return (drift[None], updated[None])


def solution(mesh):
    split = P(("group", "tm"), None, None)
    return jax.shard_map(
        per_device,
        mesh=mesh,
        in_specs=(split, split) + (P(),) * 11 + (
            P(("group", "tm"), None),
            P(("group", "tm")),
            P(("group", "tm"), None),
        ),
        out_specs=(split, split),
        check_vma=False,
    )
```

```python
import functools
import math

import jax
import jax.numpy as jnp
from jax import lax
from jax.experimental import pallas as pl
from jax.experimental.pallas import tpu as pltpu
from jax.sharding import PartitionSpec as P

HEADS = 16
CAP = 16
CHUNK = 256
LANES = 128

step_size = 0.1
inv_var = 2.0
MESH = pl.DeviceIdType.MESH
NT = (((1,), (1,)), ((), ()))
TN = (((0,), (0,)), ((), ()))


def matmul(a, b):
    return jnp.dot(a, b, preferred_element_type=jnp.float32)


def rms_norm(rows, gain):
    rows = rows.astype(jnp.float32)
    scale = lax.rsqrt(jnp.mean(rows * rows, axis=-1, keepdims=True) + 1e-05)
    return (rows * scale * gain).astype(jnp.bfloat16)


def attend(q_ref, kv_refs, out_ref, score_refs, peak_refs, parts=None, last=True):
    token_count, width = q_ref.shape
    head_size = width // HEADS
    per_block = LANES // head_size
    blocks = width // LANES
    factor = head_size ** (-0.5) * math.log2(math.e)
    lane = lax.broadcasted_iota(jnp.int32, (1, LANES), 1) // head_size
    ones = jnp.ones((16, CHUNK), jnp.bfloat16)
    chunks = [(k, v, c * CHUNK) for k, v in kv_refs for c in range(token_count // CHUNK)]

    def head_queries(block, h):
        lanes = pl.ds(pl.multiple_of(block * LANES, LANES), LANES)
        q_block = q_ref[:, lanes]
        return jnp.where(lane == h, q_block, jnp.zeros_like(q_block)), lanes

    def score(index, q_head, lanes, slot, peak):
        k, _, start = chunks[index]
        part = lax.dot_general(
            k[start : start + CHUNK, lanes], q_head, NT, preferred_element_type=jnp.float32
        )
        score_refs[slot][index * CHUNK : (index + 1) * CHUNK, :] = part
        top = jnp.max(part.reshape(CHUNK // 8, 8, token_count), axis=0)
        return top if peak is None else jnp.maximum(peak, top)

    def stage(block, h, next_block, next_h):
        slot, next_slot = h % 2, next_h % 2
        q_head, lanes = head_queries(next_block, next_h)
        largest = jnp.max(peak_refs[slot][...], axis=0, keepdims=True)
        features = pl.ds(pl.multiple_of(block * LANES + h * head_size, head_size), head_size)
        total, peak = None, None
        for index, (_, v, start) in enumerate(chunks):
            peak = score(index, q_head, lanes, next_slot, peak)
            part = score_refs[slot][index * CHUNK : (index + 1) * CHUNK, :]
            weights = jnp.exp2(((part - largest) * factor).astype(jnp.bfloat16))
            rows = jnp.concatenate([v[features, start : start + CHUNK], ones], axis=0)
            part = matmul(rows, weights)
            total = part if total is None else total + part
        peak_refs[next_slot][...] = peak
        if parts is not None:
            sums_ref, tops_ref = parts
            head = block * per_block + h
            if not last:
                sums_ref[head] = total
                tops_ref[head] = jnp.broadcast_to(largest, (8, token_count))
                return
            first = tops_ref[head][0:1]
            joint = jnp.maximum(first, largest)
            total = sums_ref[head] * jnp.exp2((first - joint) * factor) + total * jnp.exp2(
                (largest - joint) * factor
            )
        out_ref[features, :] = (
            total[:head_size] / total[head_size : head_size + 1]
        ).astype(jnp.bfloat16)

    q_head, lanes = head_queries(0, 0)
    peak = None
    for index in range(len(chunks)):
        peak = score(index, q_head, lanes, 0, peak)
    peak_refs[0][...] = peak

    @pl.loop(0, blocks)
    def _(block):
        for h in range(per_block):
            if h < per_block - 1:
                stage(block, h, block, h + 1)
            else:
                stage(block, h, jnp.minimum(block + 1, blocks - 1), 0)


def kernel(
    n,
    state_hbm, noise_hbm, gain_first, gain_second,
    wq_hbm, wk_hbm, wv_hbm, wo_hbm, cq_hbm, ck_hbm, cv_hbm, co_hbm,
    operator, owner_ref, row_ref, value_ref,
    drift_ref, updated_ref,
    x, noise, wq, wk, wv, wo, cq, ck, cv, co,
    near_rows, far_rows, normed, q, k, v, att, mid, kb, vb, message, inbox,
    scores_a, scores_b, peak_a, peak_b, sums, tops,
    load_sem, near_send, near_recv, obs_send, obs_recv,
):
    me = lax.axis_index("tm")
    token_count = x.shape[0]
    obs_count = value_ref.shape[0]

    sources = [state_hbm, wq_hbm, wk_hbm, wv_hbm, wo_hbm, cq_hbm, ck_hbm, cv_hbm, co_hbm, noise_hbm]
    targets = [x, wq, wk, wv, wo, cq, ck, cv, co, noise]
    loads = [pltpu.make_async_copy(s, t, load_sem.at[i]) for i, (s, t) in enumerate(zip(sources, targets))]
    for load in loads:
        load.start()
    load_x, load_wq, load_wk, load_wv, load_wo, load_cq, load_ck, load_cv, load_co, load_noise = loads

    barrier = pltpu.get_barrier_semaphore()

    @pl.loop(1, n)
    def _(offset):
        peer = lax.rem(me + offset, n)
        pl.semaphore_signal(barrier, inc=1, device_id={"tm": peer}, device_id_type=MESH)

    owner = owner_ref[...]
    onehot = lax.broadcasted_iota(jnp.int32, (n, obs_count), 0) == owner
    earlier = lax.broadcasted_iota(jnp.int32, (obs_count, obs_count), 0) <= lax.broadcasted_iota(
        jnp.int32, (obs_count, obs_count), 1
    )
    running = matmul(onehot.astype(jnp.bfloat16), earlier.astype(jnp.bfloat16))
    place = jnp.sum(jnp.where(onehot, running, 0.0), axis=0, keepdims=True) - 1.0
    destination = owner * CAP + place.astype(jnp.int32)
    routed = lax.broadcasted_iota(jnp.int32, (n * CAP, obs_count), 0) == destination
    values = matmul(routed.astype(jnp.bfloat16), value_ref[...])
    row = row_ref[...]
    high = jnp.sum(jnp.where(routed, ((row >> 8) + 1).astype(jnp.float32), 0.0), axis=1, keepdims=True) - 1.0
    low = jnp.sum(jnp.where(routed, (row & 255).astype(jnp.float32), 0.0), axis=1, keepdims=True)
    side = lax.broadcasted_iota(jnp.int32, (n * CAP, LANES), 1)
    codes = jnp.where(side == 0, high, low)
    message[...] = (
        jnp.concatenate([values, codes], axis=1).astype(jnp.bfloat16).reshape(message.shape)
    )

    load_x.wait()
    normed[...] = rms_norm(x[...], gain_first[...])

    pl.semaphore_wait(barrier, n - 1)
    odd = lax.rem(me, 2)
    other = me - 1 + 2 * odd
    has_other = jnp.logical_and(other >= 0, other < n)
    to_partner = pltpu.make_async_remote_copy(
        src_ref=state_hbm, dst_ref=near_rows, send_sem=near_send.at[0], recv_sem=near_recv.at[0],
        device_id={"tm": me + 1 - 2 * odd}, device_id_type=MESH,
    )
    to_other = pltpu.make_async_remote_copy(
        src_ref=state_hbm, dst_ref=far_rows, send_sem=near_send.at[1], recv_sem=near_recv.at[1],
        device_id={"tm": lax.rem(other + n, n)}, device_id_type=MESH,
    )

    @pl.when(has_other)
    def _():
        to_other.start()

    to_partner.start()

    load_wq.wait()
    q[...] = matmul(normed[...], wq[...]).astype(jnp.bfloat16)
    load_wk.wait()
    k[...] = matmul(normed[...], wk[...]).astype(jnp.bfloat16)
    load_wv.wait()
    v[...] = matmul(normed[...], wv[...]).astype(jnp.bfloat16).T

    def observation_copy(offset):
        peer = lax.rem(me + offset, n)
        return pltpu.make_async_remote_copy(
            src_ref=message.at[peer], dst_ref=inbox.at[me],
            send_sem=obs_send.at[offset], recv_sem=obs_recv.at[offset],
            device_id={"tm": peer}, device_id_type=MESH,
        )

    @pl.loop(1, n)
    def _(offset):
        observation_copy(offset).start()

    attend(q, [(k, v)], att, (scores_a, scores_b), (peak_a, peak_b))
    load_wo.wait()
    middle = (x[...].astype(jnp.float32) + lax.dot_general(att[...], wo[...], TN, preferred_element_type=jnp.float32)).astype(jnp.bfloat16)
    mid[...] = middle
    lifted = rms_norm(middle, gain_second[...])
    load_cq.wait()
    q[...] = matmul(lifted, cq[...]).astype(jnp.bfloat16)

    def project_near(rows):
        normal = rms_norm(rows[...], gain_first[...])
        kb[...] = matmul(normal, ck[...]).astype(jnp.bfloat16)
        vb[...] = matmul(normal, cv[...]).astype(jnp.bfloat16).T

    load_ck.wait()
    load_cv.wait()
    to_partner.wait()
    project_near(near_rows)
    attend(q, [(kb, vb)], att, (scores_a, scores_b), (peak_a, peak_b), (sums, tops), False)

    @pl.when(has_other)
    def _():
        to_other.wait()

    @pl.when(jnp.logical_not(has_other))
    def _():
        far_rows[...] = near_rows[...]

    project_near(far_rows)
    attend(q, [(kb, vb)], att, (scores_a, scores_b), (peak_a, peak_b), (sums, tops), True)

    @pl.loop(1, n)
    def _(offset):
        observation_copy(offset).wait()

    inbox[me] = message[me]

    arrived = inbox[...].reshape(n * CAP, 2 * LANES)
    codes_in = arrived[:, LANES:].astype(jnp.float32)
    rows_in = (codes_in[:, 0:1] * 256.0 + codes_in[:, 1:2]).astype(jnp.int32)
    hit = (rows_in == lax.broadcasted_iota(jnp.int32, (n * CAP, token_count), 1)).astype(jnp.bfloat16)
    gathered = lax.dot_general(
        hit,
        jnp.concatenate([arrived[:, :LANES], jnp.ones((n * CAP, LANES), jnp.bfloat16)], axis=1),
        TN, preferred_element_type=jnp.float32,
    )
    predicted = matmul(x[...], operator[...])
    token_misfit = (
        inv_var * (gathered[:, :LANES] - gathered[:, LANES:] * predicted)
    ).astype(jnp.bfloat16)
    gradient = lax.dot_general(token_misfit, operator[...], NT, preferred_element_type=jnp.float32)
    load_co.wait()
    combined = mid[...].astype(jnp.float32) + lax.dot_general(att[...], co[...], TN, preferred_element_type=jnp.float32) + gradient
    drift_ref[...] = combined.astype(jnp.bfloat16)
    load_noise.wait()
    updated_ref[...] = (
        x[...].astype(jnp.float32)
        + step_size * combined
        + math.sqrt(2.0 * step_size) * noise[...].astype(jnp.float32)
    ).astype(jnp.bfloat16)


def per_device(
    state, noise, gain_first, gain_second,
    self_query, self_key, self_value, self_out,
    cross_query, cross_key, cross_value, cross_out,
    obs_operator, obs_owner, obs_row, obs_value,
):
    n = lax.axis_size("tm")
    assert n % 2 == 0
    tokens = state[0]
    token_count, width = tokens.shape
    obs_count, channels = obs_value.shape
    hbm = pl.BlockSpec(memory_space=pl.ANY)
    vmem = pl.BlockSpec(memory_space=pltpu.VMEM)
    rows = pltpu.VMEM((token_count, width), jnp.bfloat16)
    square = pltpu.VMEM((width, width), jnp.bfloat16)
    box = pltpu.VMEM((n, CAP, channels + LANES), jnp.bfloat16)
    scores = pltpu.VMEM((token_count, token_count), jnp.float32)
    peak = pltpu.VMEM((8, token_count), jnp.float32)
    out = jax.ShapeDtypeStruct((token_count, width), jnp.bfloat16)
    drift, updated = pl.pallas_call(
        functools.partial(kernel, n),
        name="langevin",
        out_shape=(out, out),
        in_specs=[hbm, hbm, vmem, vmem] + [hbm] * 8 + [vmem] * 4,
        out_specs=(vmem, vmem),
        scratch_shapes=[rows, rows] + [square] * 8 + [rows] * 10 + [
            box, box,
            scores, scores, peak, peak,
            pltpu.VMEM((HEADS, width // HEADS + 16, token_count), jnp.float32),
            pltpu.VMEM((HEADS, 8, token_count), jnp.float32),
            pltpu.SemaphoreType.DMA((10,)),
            pltpu.SemaphoreType.DMA((2,)),
            pltpu.SemaphoreType.DMA((2,)),
            pltpu.SemaphoreType.DMA((n,)),
            pltpu.SemaphoreType.DMA((n,)),
        ],
        compiler_params=pltpu.CompilerParams(
            collective_id=0, has_side_effects=True, vmem_limit_bytes=56 * 1024 * 1024
        ),
    )(
        tokens, noise[0], gain_first[None, :], gain_second[None, :],
        self_query, self_key, self_value, self_out,
        cross_query, cross_key, cross_value, cross_out,
        obs_operator, obs_owner.reshape(1, obs_count), obs_row.reshape(1, obs_count), obs_value,
    )
    return (drift[None], updated[None])


def solution(mesh):
    split = P(("group", "tm"), None, None)
    return jax.shard_map(
        per_device,
        mesh=mesh,
        in_specs=(split, split) + (P(),) * 11 + (
            P(("group", "tm"), None),
            P(("group", "tm")),
            P(("group", "tm"), None),
        ),
        out_specs=(split, split),
        check_vma=False,
    )
```
